32 devices in a mesh: expert: 8 (over z, x), dp: 4 (over y, core).
Axes of the slice: x: 2, y: 2, z: 4, core: 2. Of those that a mesh axis runs over, the one named last changes fastest.
Arguments:
- tokens: bfloat16 [4096, 2048], P(('expert', 'dp')), may hold values from -6 to 6
- routes: int32 [4096, 8], P(('expert', 'dp')), may hold values from 0 to 63, all different within a row; in each aligned block of 128 rows (0 to 127, 128 to 255, ...) at most 32 rows name the same one
- gates: float32 [4096, 8], P(('expert', 'dp')), may hold values from 0.1 to 1
- cotangent: bfloat16 [4096, 2048], P(('expert', 'dp')), may hold values from -6 to 6
- w_up: bfloat16 [64, 2048, 128], P('expert'), may hold values from -0.125 to 0.125
- w_down: bfloat16 [64, 128, 2048], P('expert'), may hold values from -0.5 to 0.5
Outputs:
- mixed: bfloat16 [4096, 2048], P(('expert', 'dp'))
- token_grad: bfloat16 [4096, 2048], P(('expert', 'dp'))
- grad_up: bfloat16 [64, 2048, 128], P('expert', 'dp')
- grad_down: bfloat16 [64, 128, 2048], P('expert', None, 'dp')
The draws below stay inside these ranges and needn't reach their ends.
Inputs may be any that keep to these rules, and one draw needn't show every extreme that they name: `routes`: each row names 8 different experts; within the rows of one device no expert is named more than min(32, 128) times, and some expert is named exactly that often.
All inputs are finite; a program needn't handle non-finite values.
Results may differ from the reference program's by a relative error of at most 0.013.
Values may be sent and summed in bfloat16 or wider, within the bound.
A program may use at most 128 MiB of HBM per device.

```python
import math
import jax
import jax.numpy as jnp
import numpy as np
from jax import lax

D = 2048
F = 128
TOP = 8
TOK_DEV = 128
EXPERTS = 64
CAP = 16
TOKENS = 4096
N_EXPERT = 8
N_DP = 4


def level_of(own_key, extent, split, smallest, largest):
    def one(position, blocks):
        steps = jax.random.uniform(jax.random.fold_in(jax.random.fold_in(own_key, 6), position), (blocks,), jnp.float32, smallest / len(split), largest / len(split))
        return jnp.repeat(jnp.exp(steps), extent[position] // blocks).reshape((-1,) + (1,) * (len(extent) - position - 1))

    factor_of = one(*split[0])
    for cut in split[1:]:
        factor_of = factor_of * one(*cut)
    return factor_of


def shared_out(own_key, own, number, rows, count, top, bound, skew):
    order = jax.random.permutation(own_key, count)
    crowded, ordinary = portions_of(count, rows * top, bound, skew, True), portions_of(count, rows * top, bound, skew, False)
    places = jnp.arange(count)

    def named(sizes, turn):
        used = int((sizes > 0).sum())
        fixed = max(1, used // 4)
        moved = fixed + (places - fixed + turn * (used - fixed)) % max(1, count - fixed)
        return jnp.zeros((count,), jnp.int32).at[order[jnp.where(places < fixed, places, moved)]].set(jnp.asarray(sizes, jnp.int32))

    sizes = jnp.where(number % 4 == 0, named(crowded, number // 4), named(ordinary, number - number // 4 - 1))
    mixed = jax.random.permutation(jax.random.fold_in(own, 3), count)
    giver, taker = mixed[0:count // 2 * 2:2], mixed[1:count // 2 * 2:2]
    margin = jnp.minimum(sizes[giver] - 1, bound - sizes[taker]) // 2
    margin = jnp.where((giver == order[0]) | (taker == order[0]) | (sizes[taker] == 0), 0, jnp.maximum(margin, 0))
    moved = jax.random.randint(jax.random.fold_in(own, 4), (count // 2,), 0, 1 << 20) % (margin + 1)
    sizes = sizes.at[giver].add(-moved).at[taker].add(moved)
    members = jnp.searchsorted(jnp.cumsum(sizes), jnp.arange(rows * top), side="right").astype(jnp.int32)
    grid = members.reshape(top, rows).T
    grid = grid[jax.random.permutation(jax.random.fold_in(own, 1), rows)]
    turn = jax.random.randint(jax.random.fold_in(own, 2), (rows, 1), 0, top)
    return jnp.take_along_axis(grid, (jnp.arange(top)[None, :] + turn) % top, axis=1)


def portions_of(count, total, bound, lean, full):
    loads = [(1 << 20) // math.isqrt(rank ** lean) + 1 for rank in range(1, count + 1)]
    largest = bound if full else min(bound, max(-(-total // count), total * loads[0] // sum(loads)))
    least = 1 if total - largest >= count - 1 else 0
    counts, surplus = [largest] + [least] * (count - 1), total - largest - least * (count - 1)
    while surplus > 0:
        movable = [i for i in range(1, count) if counts[i] < largest] or [i for i in range(1, count) if counts[i] < bound]
        whole, left = sum([loads[i] for i in movable]), surplus
        for i in movable:
            extra = min(bound - counts[i], max(1, left * loads[i] // whole), surplus)
            counts[i] = counts[i] + extra
            surplus = surplus - extra
    return np.array(counts)


def scatter_about(rng, dims, deviation, most, shards=(), kind=jnp.bfloat16):
    factor_of = level_of(rng, dims, shards, -0.22, 0.18) if shards else 1.0
    values = jax.random.normal(rng, dims, jnp.float32) * deviation * factor_of
    return jnp.minimum(jnp.maximum(values, -most), most).astype(kind)


def setup_inputs(seed: int = 0) -> dict:
    streams_of = jax.random.split(jax.random.key(seed), 7)
    tokens = scatter_about(streams_of[0], (TOKENS, D), 1.0, 6.0, ((0, 32),))
    routes_keys = jax.random.split(jax.random.fold_in(streams_of[1], 1), TOKENS // TOK_DEV)
    routes_turns = jax.random.permutation(jax.random.fold_in(streams_of[1], 3), TOKENS // TOK_DEV)
    routes = jax.vmap(lambda own, number: shared_out(jax.random.fold_in(streams_of[1], 2), own, number, TOK_DEV, EXPERTS, TOP, min(2 * CAP, TOK_DEV), 2))(routes_keys, routes_turns).reshape((TOKENS, TOP))
    gates = jnp.clip(0.1 + 0.9 * jax.random.uniform(streams_of[2], (TOKENS, TOP), jnp.float32) ** level_of(streams_of[2], (TOKENS, TOP), ((0, 32),), -0.2, 0.2), 0.1, 1.0)
    cotangent = scatter_about(streams_of[3], (TOKENS, D), 1.0, 6.0, ((0, 32),))
    w_up = scatter_about(streams_of[4], (EXPERTS, D, F), D ** -0.5, 0.125, ((0, 8),))
    w_down = scatter_about(streams_of[5], (EXPERTS, F, D), F ** -0.5, 0.5, ((0, 8),))
    return dict(tokens=tokens, routes=routes, gates=gates, cotangent=cotangent, w_up=w_up, w_down=w_down)


gelu_coef = 0.7978845608028654
cubic_coef = 0.044715


def tanh_gelu(pre_act):
    inner_arg = gelu_coef * (pre_act + cubic_coef * pre_act * pre_act * pre_act)
    return 0.5 * pre_act * (1.0 + jnp.tanh(inner_arg))


def tanh_gelu_slope(pre_act):
    inner_arg = gelu_coef * (pre_act + cubic_coef * pre_act * pre_act * pre_act)
    tanh_part = jnp.tanh(inner_arg)
    return 0.5 * (1.0 + tanh_part) + 0.5 * pre_act * (1.0 - tanh_part * tanh_part) * gelu_coef * (1.0 + 3.0 * cubic_coef * pre_act * pre_act)


def route_ranks(flat_routes):
    positions = jnp.arange(flat_routes.shape[0], dtype=jnp.int32)
    matches = (flat_routes[None, :] == flat_routes[:, None]) & (positions[None, :] < positions[:, None])
    return jnp.sum(matches.astype(jnp.int32), axis=1)


def slot_table(flat_routes, experts_all, capacity):
    route_total = flat_routes.shape[0]
    ranking = route_ranks(flat_routes)
    kept_mask = ranking < capacity
    slot_index = jnp.where(kept_mask, flat_routes * capacity + ranking, experts_all * capacity).astype(jnp.int32)
    slot_route = jnp.full((experts_all * capacity + 1,), -1, jnp.int32)
    slot_route = slot_route.at[slot_index].set(jnp.arange(route_total, dtype=jnp.int32))
    return slot_route[:-1], kept_mask, slot_index


def reference(tokens, routes, gates, cotangent, w_up, w_down):
    block_total = N_EXPERT * N_DP
    route_block = TOK_DEV * TOP
    block_routes = routes.reshape(block_total, route_block)

    def per_block(one_block):
        slot_route, kept_mask, slot_index = slot_table(one_block, EXPERTS, CAP)
        return slot_route

    slot_route = lax.map(per_block, block_routes)
    block_base = (jnp.arange(block_total, dtype=jnp.int32) * route_block)[:, None]
    global_route = jnp.where(slot_route >= 0, slot_route + block_base, -1).astype(jnp.int32)
    per_expert = global_route.reshape(block_total, EXPERTS, CAP).transpose(1, 0, 2).reshape(EXPERTS, block_total * CAP)
    flat_gates = gates.reshape(-1)

    def expert_step(carry, inputs):
        mixed_acc, grad_acc = carry
        route_ids, up_mat, down_mat = inputs
        slot_valid = route_ids >= 0
        safe_route = jnp.where(slot_valid, route_ids, 0)
        token_ids = safe_route // TOP
        rows_in = jnp.where(slot_valid[:, None], tokens[token_ids], jnp.zeros((), jnp.bfloat16))
        gate_vals = jnp.where(slot_valid, flat_gates[safe_route], jnp.float32(0.0))
        slot_grads = (gate_vals[:, None] * cotangent[token_ids].astype(jnp.float32)).astype(jnp.bfloat16)
        pre_act = jnp.dot(rows_in, up_mat, preferred_element_type=jnp.float32)
        hidden = tanh_gelu(pre_act).astype(jnp.bfloat16)
        expert_out = jnp.dot(hidden, down_mat, preferred_element_type=jnp.float32).astype(jnp.bfloat16)
        mixed_acc = mixed_acc.at[token_ids].add(gate_vals[:, None] * expert_out.astype(jnp.float32))
        grad_hidden = jnp.dot(slot_grads, down_mat.T, preferred_element_type=jnp.float32)
        grad_pre = (grad_hidden * tanh_gelu_slope(pre_act)).astype(jnp.bfloat16)
        grad_rows = jnp.dot(grad_pre, up_mat.T, preferred_element_type=jnp.float32).astype(jnp.bfloat16)
        grad_acc = grad_acc.at[token_ids].add(grad_rows.astype(jnp.float32))
        rows_split = rows_in.reshape(N_EXPERT, N_DP, CAP, D).astype(jnp.float32)
        pre_split = grad_pre.reshape(N_EXPERT, N_DP, CAP, F).astype(jnp.float32)
        hidden_split = hidden.reshape(N_EXPERT, N_DP, CAP, F).astype(jnp.float32)
        grads_split = slot_grads.reshape(N_EXPERT, N_DP, CAP, D).astype(jnp.float32)
        part_up = jnp.einsum("apcd,apcf->pdf", rows_split, pre_split)
        part_down = jnp.einsum("apcf,apcd->pfd", hidden_split, grads_split)
        part_up = lax.optimization_barrier(part_up.astype(jnp.bfloat16))
        part_down = lax.optimization_barrier(part_down.astype(jnp.bfloat16))
        up_total = jnp.sum(part_up.astype(jnp.float32), axis=0).astype(jnp.bfloat16)
        down_total = jnp.sum(part_down.astype(jnp.float32), axis=0).astype(jnp.bfloat16)
        return (mixed_acc, grad_acc), (up_total, down_total)

    start_mixed = jnp.zeros((TOKENS, D), jnp.float32)
    start_grad = jnp.zeros((TOKENS, D), jnp.float32)
    carried, stacked = lax.scan(expert_step, (start_mixed, start_grad), (per_expert, w_up, w_down))
    mixed_acc, grad_acc = carried
    grad_up, grad_down = stacked
    mixed = (tokens.astype(jnp.float32) + mixed_acc).astype(jnp.bfloat16)
    token_grad = (cotangent.astype(jnp.float32) + grad_acc).astype(jnp.bfloat16)
    return mixed, token_grad, grad_up, grad_down
```

```python
import jax
import jax.numpy as jnp
from jax import lax
from jax.sharding import PartitionSpec as P

gelu_coef = 0.7978845608028654
cubic_coef = 0.044715


def gelu_and_slope(pre_act):
    square = pre_act * pre_act
    tanh_part = jnp.tanh(gelu_coef * pre_act * (1.0 + cubic_coef * square))
    value = 0.5 * pre_act * (1.0 + tanh_part)
    slope = 0.5 * (1.0 + tanh_part) + 0.5 * pre_act * (1.0 - tanh_part * tanh_part) * gelu_coef * (
        1.0 + 3.0 * cubic_coef * square
    )
    return value, slope


def kept_gates(routes, gates, experts_all, capacity):
    tok_rows = routes.shape[0]
    hits = routes[:, :, None] == jnp.arange(experts_all, dtype=jnp.int32)[None, None, :]
    named = jnp.any(hits, axis=1)
    gate_of = jnp.sum(jnp.where(hits, gates[:, :, None], jnp.float32(0.0)), axis=1)
    earlier = jnp.tril(jnp.ones((tok_rows, tok_rows), jnp.bfloat16), -1)
    rank = jnp.dot(earlier, named.astype(jnp.bfloat16), preferred_element_type=jnp.float32)
    return jnp.where(named & (rank < capacity), gate_of, jnp.float32(0.0))


def per_device(tokens, routes, gates, cotangent, w_up, w_down):
    n_expert = lax.axis_size("expert")
    local_experts, model_width, hidden_width = w_up.shape
    experts_all = local_experts * n_expert
    tok_rows = tokens.shape[0]
    top_k = routes.shape[1]
    capacity = tok_rows * top_k // experts_all
    rows_all = n_expert * tok_rows
    units = local_experts * hidden_width

    gate_full = kept_gates(routes, gates, experts_all, capacity)
    gate_hi = gate_full.astype(jnp.bfloat16)
    gate_lo = (gate_full - gate_hi.astype(jnp.float32)).astype(jnp.bfloat16)
    gate_pair = jnp.concatenate([gate_hi, gate_lo], axis=1)

    all_tokens = lax.all_gather(tokens, "expert", axis=0, tiled=True)
    all_cot = lax.all_gather(
        jnp.concatenate([cotangent, gate_pair], axis=1), "expert", axis=0, tiled=True
    )
    first = lax.axis_index("expert") * local_experts
    all_gates = lax.dynamic_slice_in_dim(
        all_cot, model_width + first, local_experts, axis=1
    ).astype(jnp.float32) + lax.dynamic_slice_in_dim(
        all_cot, model_width + experts_all + first, local_experts, axis=1
    ).astype(jnp.float32)
    all_cot = all_cot[:, :model_width]
    gate_units = all_gates[:, :, None]

    pre_act = jnp.einsum("td,edf->tef", all_tokens, w_up, preferred_element_type=jnp.float32)
    value, slope = gelu_and_slope(pre_act)
    weighted = (value * gate_units).astype(jnp.bfloat16)
    mixed_part = jnp.einsum(
        "tef,efd->td", weighted, w_down, preferred_element_type=jnp.float32
    ).astype(jnp.bfloat16)
    mixed_sum = lax.psum_scatter(mixed_part, "expert", scatter_dimension=0, tiled=True)

    grad_hidden = jnp.einsum("td,efd->tef", all_cot, w_down, preferred_element_type=jnp.float32)
    grad_pre = (grad_hidden * slope * gate_units).astype(jnp.bfloat16)
    grad_part = jnp.einsum(
        "tef,edf->td", grad_pre, w_up, preferred_element_type=jnp.float32
    ).astype(jnp.bfloat16)
    grad_sum = lax.psum_scatter(grad_part, "expert", scatter_dimension=0, tiled=True)

    part_up = jnp.einsum(
        "td,tef->edf", all_tokens, grad_pre, preferred_element_type=jnp.float32
    ).astype(jnp.bfloat16)
    part_down = jnp.einsum(
        "tef,td->efd", weighted, all_cot, preferred_element_type=jnp.float32
    ).astype(jnp.bfloat16)
    up_sum = lax.psum_scatter(part_up, "dp", scatter_dimension=1, tiled=True)
    down_sum = lax.psum_scatter(part_down, "dp", scatter_dimension=2, tiled=True)

    mixed = (tokens.astype(jnp.float32) + mixed_sum.astype(jnp.float32)).astype(jnp.bfloat16)
    token_grad = (cotangent.astype(jnp.float32) + grad_sum.astype(jnp.float32)).astype(
        jnp.bfloat16
    )
    return (mixed, token_grad, up_sum, down_sum)


def solution(mesh):
    return jax.shard_map(
        per_device,
        mesh=mesh,
        in_specs=(
            P(("expert", "dp"), None),
            P(("expert", "dp"), None),
            P(("expert", "dp"), None),
            P(("expert", "dp"), None),
            P("expert", None, None),
            P("expert", None, None),
        ),
        out_specs=(
            P(("expert", "dp"), None),
            P(("expert", "dp"), None),
            P("expert", "dp", None),
            P("expert", None, "dp"),
        ),
        check_vma=False,
    )
```

```python
import jax
import jax.numpy as jnp
from jax import lax
from jax.sharding import PartitionSpec as P


gelu_coef = 0.7978845608028654
cubic_coef = 0.044715


def gelu_and_slope(pre_act):
    square = pre_act * pre_act
    tanh_part = jnp.tanh(gelu_coef * pre_act * (1.0 + cubic_coef * square))
    value = 0.5 * pre_act * (1.0 + tanh_part)
    slope = 0.5 * (1.0 + tanh_part) + 0.5 * pre_act * (1.0 - tanh_part * tanh_part) * gelu_coef * (
        1.0 + 3.0 * cubic_coef * square
    )
    return value, slope


def kept_gates(routes, gates, experts_all, capacity):
    tok_rows = routes.shape[0]
    hits = routes[:, :, None] == jnp.arange(experts_all, dtype=jnp.int32)[None, None, :]
    named = jnp.any(hits, axis=1)
    gate_of = jnp.sum(jnp.where(hits, gates[:, :, None], jnp.float32(0.0)), axis=1)
    earlier = jnp.tril(jnp.ones((tok_rows, tok_rows), jnp.bfloat16), -1)
    rank = jnp.dot(earlier, named.astype(jnp.bfloat16), preferred_element_type=jnp.float32)
    return jnp.where(named & (rank < capacity), gate_of, jnp.float32(0.0))


def shifted(value, axis, table):
    return lax.ppermute(value, axis, table)


def after(value, *others):
    return lax.optimization_barrier((value,) + others)[0]


def shift_table(outer, inner, outer_by, inner_by):
    pairs = []
    for a in range(outer):
        for b in range(inner):
            to = (a + outer_by) % outer * inner + (b + inner_by) % inner
            pairs.append((a * inner + b, to))
    return pairs


def per_device(tokens, routes, gates, cotangent, w_up, w_down):
    n_expert, n_dp = lax.axis_size("expert"), lax.axis_size("dp")
    cores = 2
    n_x = n_dp // cores
    n_z = n_expert // n_x
    local_experts, model_width, _ = w_up.shape
    experts_all = local_experts * n_expert
    tok_rows = tokens.shape[0]
    top_k = routes.shape[1]
    capacity = tok_rows * top_k // experts_all
    first = lax.axis_index("expert") * local_experts

    def z_shift(block, by):
        return shifted(block, "expert", shift_table(n_z, n_x, by, 0))

    def x_shift(block, by):
        return shifted(block, "expert", shift_table(n_z, n_x, 0, by))

    z_order = sorted(range(1, n_z), key=lambda by: min(by, n_z - by))

    def gather_both(rows, cots):
        row_of, cot_of = {(0, 0): rows}, {(0, 0): cots}
        for sx in range(1, n_x):
            row_of[sx, 0] = x_shift(rows, sx)
            cot_of[sx, 0] = x_shift(after(cots, row_of[sx, 0]), sx)
        for by in z_order:
            row_of[0, by] = z_shift(rows, by)
        near, far = z_order[:-1], z_order[-1]
        for by in near:
            cot_of[0, by] = z_shift(after(cots, *[row_of[0, b] for b in near]), by)
        last = cot_of[n_x - 1, 0]
        for by in z_order:
            for sx in range(1, n_x):
                row_of[sx, by] = x_shift(after(row_of[0, by], last), sx)
        cot_of[0, far] = z_shift(after(cots, row_of[0, far]), far)
        for by in z_order:
            for sx in range(1, n_x):
                cot_of[sx, by] = x_shift(cot_of[0, by], sx)
        for part in (row_of, cot_of):
            part[0, far] = after(part[0, far], *[part[n_x - 1, by] for by in near])
        return [
            [
                jnp.concatenate([part[sx, sz] for sz in range(n_z)], axis=0)
                for sx in range(n_x)
            ]
            for part in (row_of, cot_of)
        ]

    def scatter(parts):
        def total(sz, *earlier):
            rows = slice(sz * tok_rows, (sz + 1) * tok_rows)
            value = parts[0][rows].astype(jnp.float32)
            for item in sent[sz]:
                value = value + after(item, *earlier).astype(jnp.float32)
            return value

        sent = {}
        for sz in z_order + [0]:
            rows = slice(sz * tok_rows, (sz + 1) * tok_rows)
            sent[sz] = [x_shift(parts[sx][rows], -sx) for sx in range(1, n_x)]
        arrived = []
        for sz in z_order:
            column = total(sz, *arrived[-1:]).astype(jnp.bfloat16)
            arrived.append(z_shift(column, -sz))
        return total(0), arrived

    def summed(own, arrived):
        for item in arrived:
            own = own + item.astype(jnp.float32)
        return own

    def reduce_dp(part, axis):
        n_y = n_dp // cores
        core = lax.axis_index("dp") % cores
        level = lax.axis_index("dp") // cores
        width = part.shape[axis] // n_dp

        def piece(y, c):
            return lax.dynamic_slice_in_dim(part, (y * cores + c) * width, width, axis)

        sums = []
        for sy in range(n_y):
            y = (level + sy) % n_y
            sent = shifted(piece(y, 1 - core), "dp", shift_table(n_y, cores, 0, 1))
            sums.append(piece(y, core).astype(jnp.float32) + sent.astype(jnp.float32))
        result = sums[0]
        for sy in range(1, n_y):
            sent = shifted(
                sums[sy].astype(jnp.bfloat16), "dp", shift_table(n_y, cores, sy, 0)
            )
            result = result + sent.astype(jnp.float32)
        return result.astype(jnp.bfloat16)

    gate_full = kept_gates(routes, gates, experts_all, capacity)
    gate_hi = gate_full.astype(jnp.bfloat16)
    gate_lo = (gate_full - gate_hi.astype(jnp.float32)).astype(jnp.bfloat16)
    with_gates, cots = gather_both(
        jnp.concatenate([tokens, gate_hi, gate_lo], axis=1), cotangent
    )

    slopes, weights_of, rows_of, mixed_parts = [], [], [], []
    for chunk in with_gates:
        gate_units = (
            lax.dynamic_slice_in_dim(chunk, model_width + first, local_experts, axis=1).astype(
                jnp.float32
            )
            + lax.dynamic_slice_in_dim(
                chunk, model_width + experts_all + first, local_experts, axis=1
            ).astype(jnp.float32)
        )[:, :, None]
        rows = chunk[:, :model_width]
        pre_act = jnp.einsum("td,edf->tef", rows, w_up, preferred_element_type=jnp.float32)
        value, slope = gelu_and_slope(pre_act)
        weighted = (value * gate_units).astype(jnp.bfloat16)
        mixed_parts.append(
            jnp.einsum("tef,efd->td", weighted, w_down, preferred_element_type=jnp.float32).astype(
                jnp.bfloat16
            )
        )
        slopes.append(slope * gate_units)
        weights_of.append(weighted)
        rows_of.append(rows)
    mixed_own, mixed_arrived = scatter(mixed_parts)
    mixed_sum = summed(mixed_own, mixed_arrived)

    grad_pres, grad_parts = [], []
    for slope, rows in zip(slopes, cots):
        grad_hidden = jnp.einsum("td,efd->tef", rows, w_down, preferred_element_type=jnp.float32)
        grad_pre = (grad_hidden * slope).astype(jnp.bfloat16)
        grad_parts.append(
            jnp.einsum("tef,edf->td", grad_pre, w_up, preferred_element_type=jnp.float32).astype(
                jnp.bfloat16
            )
        )
        grad_pres.append(grad_pre)
    grad_own, grad_arrived = scatter(grad_parts)
    grad_sum = summed(grad_own, grad_arrived)

    weights_of = [after(item, mixed_arrived[0]) for item in weights_of]
    rows_of = [after(item, mixed_arrived[0]) for item in rows_of]

    part_down = sum(
        jnp.einsum("tef,td->efd", a, b, preferred_element_type=jnp.float32)
        for a, b in zip(weights_of, cots)
    ).astype(jnp.bfloat16)
    part_up = sum(
        jnp.einsum("td,tef->edf", a, b, preferred_element_type=jnp.float32)
        for a, b in zip(rows_of, grad_pres)
    ).astype(jnp.bfloat16)
    down_sum = reduce_dp(part_down, 2)
    up_sum = reduce_dp(part_up, 1)

    mixed = (tokens.astype(jnp.float32) + mixed_sum).astype(jnp.bfloat16)
    token_grad = (cotangent.astype(jnp.float32) + grad_sum).astype(jnp.bfloat16)
    return (mixed, token_grad, up_sum, down_sum)


def per_device_wide(tokens, routes, gates, cotangent, w_up, w_down):
    n_expert = lax.axis_size("expert")
    local_experts, model_width, _ = w_up.shape
    experts_all = local_experts * n_expert
    tok_rows = tokens.shape[0]
    top_k = routes.shape[1]
    capacity = tok_rows * top_k // experts_all

    gate_full = kept_gates(routes, gates, experts_all, capacity)
    gate_hi = gate_full.astype(jnp.bfloat16)
    gate_lo = (gate_full - gate_hi.astype(jnp.float32)).astype(jnp.bfloat16)
    gate_pair = jnp.concatenate([gate_hi, gate_lo], axis=1)

    all_tokens = lax.all_gather(tokens, "expert", axis=0, tiled=True)
    all_cot = lax.all_gather(
        jnp.concatenate([cotangent, gate_pair], axis=1), "expert", axis=0, tiled=True
    )
    first = lax.axis_index("expert") * local_experts
    all_gates = lax.dynamic_slice_in_dim(
        all_cot, model_width + first, local_experts, axis=1
    ).astype(jnp.float32) + lax.dynamic_slice_in_dim(
        all_cot, model_width + experts_all + first, local_experts, axis=1
    ).astype(jnp.float32)
    all_cot = all_cot[:, :model_width]
    gate_units = all_gates[:, :, None]

    pre_act = jnp.einsum("td,edf->tef", all_tokens, w_up, preferred_element_type=jnp.float32)
    value, slope = gelu_and_slope(pre_act)
    weighted = (value * gate_units).astype(jnp.bfloat16)
    mixed_part = jnp.einsum(
        "tef,efd->td", weighted, w_down, preferred_element_type=jnp.float32
    ).astype(jnp.bfloat16)
    mixed_sum = lax.psum_scatter(mixed_part, "expert", scatter_dimension=0, tiled=True)

    grad_hidden = jnp.einsum("td,efd->tef", all_cot, w_down, preferred_element_type=jnp.float32)
    grad_pre = (grad_hidden * slope * gate_units).astype(jnp.bfloat16)
    grad_part = jnp.einsum(
        "tef,edf->td", grad_pre, w_up, preferred_element_type=jnp.float32
    ).astype(jnp.bfloat16)
    grad_sum = lax.psum_scatter(grad_part, "expert", scatter_dimension=0, tiled=True)

    part_up = jnp.einsum(
        "td,tef->edf", all_tokens, grad_pre, preferred_element_type=jnp.float32
    ).astype(jnp.bfloat16)
    part_down = jnp.einsum(
        "tef,td->efd", weighted, all_cot, preferred_element_type=jnp.float32
    ).astype(jnp.bfloat16)
    up_sum = lax.psum_scatter(part_up, "dp", scatter_dimension=1, tiled=True)
    down_sum = lax.psum_scatter(part_down, "dp", scatter_dimension=2, tiled=True)

    mixed = (tokens.astype(jnp.float32) + mixed_sum.astype(jnp.float32)).astype(jnp.bfloat16)
    token_grad = (cotangent.astype(jnp.float32) + grad_sum.astype(jnp.float32)).astype(
        jnp.bfloat16
    )
    return (mixed, token_grad, up_sum, down_sum)


def solution(mesh):
    small = mesh.shape["expert"] <= 8
    return jax.shard_map(
        per_device if small else per_device_wide,
        mesh=mesh,
        in_specs=(
            P(("expert", "dp"), None),
            P(("expert", "dp"), None),
            P(("expert", "dp"), None),
            P(("expert", "dp"), None),
            P("expert", None, None),
            P("expert", None, None),
        ),
        out_specs=(
            P(("expert", "dp"), None),
            P(("expert", "dp"), None),
            P("expert", "dp", None),
            P("expert", None, "dp"),
        ),
        check_vma=False,
    )
```

```python
import jax
import jax.numpy as jnp
from jax import lax
from jax.sharding import PartitionSpec as P


gelu_coef = 0.7978845608028654
cubic_coef = 0.044715


def gelu_and_slope(pre_act):
    square = pre_act * pre_act
    tanh_part = jnp.tanh(gelu_coef * pre_act * (1.0 + cubic_coef * square))
    value = 0.5 * pre_act * (1.0 + tanh_part)
    slope = 0.5 * (1.0 + tanh_part) + 0.5 * pre_act * (1.0 - tanh_part * tanh_part) * gelu_coef * (
        1.0 + 3.0 * cubic_coef * square
    )
    return value, slope


def kept_gates(routes, gates, experts_all, capacity):
    tok_rows = routes.shape[0]
    hits = routes[:, :, None] == jnp.arange(experts_all, dtype=jnp.int32)[None, None, :]
    named = jnp.any(hits, axis=1)
    gate_of = jnp.sum(jnp.where(hits, gates[:, :, None], jnp.float32(0.0)), axis=1)
    earlier = jnp.tril(jnp.ones((tok_rows, tok_rows), jnp.bfloat16), -1)
    rank = jnp.dot(earlier, named.astype(jnp.bfloat16), preferred_element_type=jnp.float32)
    return jnp.where(named & (rank < capacity), gate_of, jnp.float32(0.0))


def shifted(value, axis, table):
    return lax.ppermute(value, axis, table)


def after(value, *others):
    return lax.optimization_barrier((value,) + others)[0]


def shift_table(outer, inner, outer_by, inner_by):
    pairs = []
    for a in range(outer):
        for b in range(inner):
            to = (a + outer_by) % outer * inner + (b + inner_by) % inner
            pairs.append((a * inner + b, to))
    return pairs


def per_device(tokens, routes, gates, cotangent, w_up, w_down):
    n_expert, n_dp = lax.axis_size("expert"), lax.axis_size("dp")
    cores = 2
    n_x = n_dp // cores
    n_z = n_expert // n_x
    local_experts, model_width, _ = w_up.shape
    experts_all = local_experts * n_expert
    tok_rows = tokens.shape[0]
    top_k = routes.shape[1]
    capacity = tok_rows * top_k // experts_all
    first = lax.axis_index("expert") * local_experts

    def z_shift(block, by):
        return shifted(block, "expert", shift_table(n_z, n_x, by, 0))

    def x_shift(block, by):
        return shifted(block, "expert", shift_table(n_z, n_x, 0, by))

    z_order = sorted(range(1, n_z), key=lambda by: min(by, n_z - by))

    def gather_both(rows, cots):
        row_of, cot_of = {(0, 0): rows}, {(0, 0): cots}
        for sx in range(1, n_x):
            row_of[sx, 0] = x_shift(rows, sx)
            cot_of[sx, 0] = x_shift(after(cots, row_of[sx, 0]), sx)
        for by in z_order:
            row_of[0, by] = z_shift(rows, by)
        near, far = z_order[:-1], z_order[-1]
        for by in near:
            cot_of[0, by] = z_shift(after(cots, row_of[0, far]), by)
        for by in z_order:
            for sx in range(1, n_x):
                row_of[sx, by] = x_shift(row_of[0, by], sx)
        cot_of[0, far] = z_shift(after(cots, row_of[0, far]), far)
        for by in z_order:
            for sx in range(1, n_x):
                cot_of[sx, by] = x_shift(cot_of[0, by], sx)
        for part in (row_of, cot_of):
            part[0, far] = after(part[0, far], *[part[n_x - 1, by] for by in near])
        cot_of[0, 0] = after(cots, row_of[n_x - 1, far])
        return [
            [
                jnp.concatenate([part[sx, sz] for sz in range(n_z)], axis=0)
                for sx in range(n_x)
            ]
            for part in (row_of, cot_of)
        ]

    def scatter(parts, name):
        def total(sz, *earlier):
            rows = slice(sz * tok_rows, (sz + 1) * tok_rows)
            value = parts[0][rows].astype(jnp.float32)
            for item in sent[sz]:
                value = value + after(item, *earlier).astype(jnp.float32)
            return value

        sent = {}
        for sz in z_order + [0]:
            rows = slice(sz * tok_rows, (sz + 1) * tok_rows)
            sent[sz] = [x_shift(parts[sx][rows], -sx) for sx in range(1, n_x)]
        arrived = []
        for sz in z_order:
            column = total(sz, *(arrived[-1:] if name == "m" else arrived[:1])).astype(jnp.bfloat16)
            arrived.append(z_shift(column, -sz))
        return total(0, arrived[-1]), arrived

    def summed(own, arrived):
        for item in arrived:
            own = own + item.astype(jnp.float32)
        return own

    def reduce_dp(part, axis):
        n_y = n_dp // cores
        core = lax.axis_index("dp") % cores
        level = lax.axis_index("dp") // cores
        width = part.shape[axis] // n_dp

        def piece(y, c):
            return lax.dynamic_slice_in_dim(part, (y * cores + c) * width, width, axis)

        sums = []
        for sy in range(n_y):
            y = (level + sy) % n_y
            sent = shifted(piece(y, 1 - core), "dp", shift_table(n_y, cores, 0, 1))
            sums.append(piece(y, core).astype(jnp.float32) + sent.astype(jnp.float32))
        result = sums[0]
        for sy in range(1, n_y):
            sent = shifted(
                sums[sy].astype(jnp.bfloat16), "dp", shift_table(n_y, cores, sy, 0)
            )
            result = result + sent.astype(jnp.float32)
        return result.astype(jnp.bfloat16)

    gate_full = kept_gates(routes, gates, experts_all, capacity)
    gate_hi = gate_full.astype(jnp.bfloat16)
    gate_lo = (gate_full - gate_hi.astype(jnp.float32)).astype(jnp.bfloat16)
    with_gates, cots = gather_both(
        jnp.concatenate([tokens, gate_hi, gate_lo], axis=1), cotangent
    )

    slopes, weights_of, rows_of, mixed_parts = [], [], [], []
    for chunk in with_gates:
        gate_units = (
            lax.dynamic_slice_in_dim(chunk, model_width + first, local_experts, axis=1).astype(
                jnp.float32
            )
            + lax.dynamic_slice_in_dim(
                chunk, model_width + experts_all + first, local_experts, axis=1
            ).astype(jnp.float32)
        )[:, :, None]
        rows = chunk[:, :model_width]
        pre_act = jnp.einsum("td,edf->tef", rows, w_up, preferred_element_type=jnp.float32)
        value, slope = gelu_and_slope(pre_act)
        weighted = (value * gate_units).astype(jnp.bfloat16)
        mixed_parts.append(
            jnp.einsum("tef,efd->td", weighted, w_down, preferred_element_type=jnp.float32).astype(
                jnp.bfloat16
            )
        )
        slopes.append(slope * gate_units)
        weights_of.append(weighted)
        rows_of.append(rows)
    mixed_own, mixed_arrived = scatter(mixed_parts, "m")
    mixed_sum = summed(mixed_own, mixed_arrived)

    grad_pres, grad_parts = [], []
    for slope, rows in zip(slopes, cots):
        grad_hidden = jnp.einsum("td,efd->tef", rows, w_down, preferred_element_type=jnp.float32)
        grad_pre = (grad_hidden * slope).astype(jnp.bfloat16)
        grad_parts.append(
            jnp.einsum("tef,edf->td", grad_pre, w_up, preferred_element_type=jnp.float32).astype(
                jnp.bfloat16
            )
        )
        grad_pres.append(grad_pre)
    grad_own, grad_arrived = scatter(grad_parts, "g")
    grad_sum = summed(grad_own, grad_arrived)

    weights_of = [after(item, mixed_arrived[0]) for item in weights_of]
    rows_of = [after(item, mixed_arrived[0]) for item in rows_of]

    part_down = sum(
        jnp.einsum("tef,td->efd", a, b, preferred_element_type=jnp.float32)
        for a, b in zip(weights_of, cots)
    ).astype(jnp.bfloat16)
    part_up = sum(
        jnp.einsum("td,tef->edf", a, b, preferred_element_type=jnp.float32)
        for a, b in zip(rows_of, grad_pres)
    ).astype(jnp.bfloat16)
    down_sum = reduce_dp(part_down, 2)
    up_sum = reduce_dp(part_up, 1)

    mixed = (tokens.astype(jnp.float32) + mixed_sum).astype(jnp.bfloat16)
    token_grad = (cotangent.astype(jnp.float32) + grad_sum).astype(jnp.bfloat16)
    return (mixed, token_grad, up_sum, down_sum)


def per_device_wide(tokens, routes, gates, cotangent, w_up, w_down):
    n_expert = lax.axis_size("expert")
    local_experts, model_width, _ = w_up.shape
    experts_all = local_experts * n_expert
    tok_rows = tokens.shape[0]
    top_k = routes.shape[1]
    capacity = tok_rows * top_k // experts_all

    gate_full = kept_gates(routes, gates, experts_all, capacity)
    gate_hi = gate_full.astype(jnp.bfloat16)
    gate_lo = (gate_full - gate_hi.astype(jnp.float32)).astype(jnp.bfloat16)
    gate_pair = jnp.concatenate([gate_hi, gate_lo], axis=1)

    all_tokens = lax.all_gather(tokens, "expert", axis=0, tiled=True)
    all_cot = lax.all_gather(
        jnp.concatenate([cotangent, gate_pair], axis=1), "expert", axis=0, tiled=True
    )
    first = lax.axis_index("expert") * local_experts
    all_gates = lax.dynamic_slice_in_dim(
        all_cot, model_width + first, local_experts, axis=1
    ).astype(jnp.float32) + lax.dynamic_slice_in_dim(
        all_cot, model_width + experts_all + first, local_experts, axis=1
    ).astype(jnp.float32)
    all_cot = all_cot[:, :model_width]
    gate_units = all_gates[:, :, None]

    pre_act = jnp.einsum("td,edf->tef", all_tokens, w_up, preferred_element_type=jnp.float32)
    value, slope = gelu_and_slope(pre_act)
    weighted = (value * gate_units).astype(jnp.bfloat16)
    mixed_part = jnp.einsum(
        "tef,efd->td", weighted, w_down, preferred_element_type=jnp.float32
    ).astype(jnp.bfloat16)
    mixed_sum = lax.psum_scatter(mixed_part, "expert", scatter_dimension=0, tiled=True)

    grad_hidden = jnp.einsum("td,efd->tef", all_cot, w_down, preferred_element_type=jnp.float32)
    grad_pre = (grad_hidden * slope * gate_units).astype(jnp.bfloat16)
    grad_part = jnp.einsum(
        "tef,edf->td", grad_pre, w_up, preferred_element_type=jnp.float32
    ).astype(jnp.bfloat16)
    grad_sum = lax.psum_scatter(grad_part, "expert", scatter_dimension=0, tiled=True)

    part_up = jnp.einsum(
        "td,tef->edf", all_tokens, grad_pre, preferred_element_type=jnp.float32
    ).astype(jnp.bfloat16)
    part_down = jnp.einsum(
        "tef,td->efd", weighted, all_cot, preferred_element_type=jnp.float32
    ).astype(jnp.bfloat16)
    up_sum = lax.psum_scatter(part_up, "dp", scatter_dimension=1, tiled=True)
    down_sum = lax.psum_scatter(part_down, "dp", scatter_dimension=2, tiled=True)

    mixed = (tokens.astype(jnp.float32) + mixed_sum.astype(jnp.float32)).astype(jnp.bfloat16)
    token_grad = (cotangent.astype(jnp.float32) + grad_sum.astype(jnp.float32)).astype(
        jnp.bfloat16
    )
    return (mixed, token_grad, up_sum, down_sum)


def solution(mesh):
    small = mesh.shape["expert"] <= 8
    return jax.shard_map(
        per_device if small else per_device_wide,
        mesh=mesh,
        in_specs=(
            P(("expert", "dp"), None),
            P(("expert", "dp"), None),
            P(("expert", "dp"), None),
            P(("expert", "dp"), None),
            P("expert", None, None),
            P("expert", None, None),
        ),
        out_specs=(
            P(("expert", "dp"), None),
            P(("expert", "dp"), None),
            P("expert", "dp", None),
            P("expert", None, "dp"),
        ),
        check_vma=False,
    )
```
